32 devices in a mesh: section: 4 (over x, core), row: 4 (over z), col: 2 (over y).
Axes of the slice: x: 2, y: 2, z: 4, core: 2. Of those that a mesh axis runs over, the one named last changes fastest.
Arguments:
- latents: bfloat16 [2, 1280, 4, 128], P(None, 'col', 'row'), may hold values from -6 to 6
- timesteps: int32 [2], replicated, may hold values from 0 to 999
- weights: bfloat16 [4, 1280, 1280], P('section', 'row', 'col'), may hold values from -0.15625 to 0.15625
- taps: float32 [4, 3, 1280], P('section'), may hold values from -3 to 3
- time_table: bfloat16 [4, 1000, 1280], P('section'), may hold values from -5 to 5
- dilations: int32 [4], P('section'), may hold values from 1 to 4
Outputs:
- acts: bfloat16 [4, 2, 1280, 4, 128], P('section', None, 'col', 'row')
The draws below stay inside these ranges and needn't reach their ends.
All inputs are finite; a program needn't handle non-finite values.
Results may differ from the reference program's by a relative error of at most 0.03.
Values may be sent and summed in bfloat16 or wider, within the bound.
A program may use at most 64 MiB of HBM per device.

```python
import jax
import jax.numpy as jnp
from jax import lax

CH = 1280
FRAMES = 128
MICRO = 2
NSTEPS = 1000
DMAX = 4
POSITIONS = 4
LEVELS = 4


def plant(values, stream_key, low, largest):
    longest = values.shape.index(max(values.shape))
    spots = []
    for shift in (0, 1):
        where = [jax.random.randint(jax.random.fold_in(stream_key, axis), (), 0, length) for axis, length in enumerate(values.shape)]
        where[longest] = (where[longest] + shift) % values.shape[longest]
        spots.append(tuple(where))
    return values.at[spots[0]].set(low).at[spots[1]].set(largest)


def block_scale(stream_key, extent, pieces, least, top_value):
    def one(dim, blocks):
        heights = jax.random.uniform(jax.random.fold_in(jax.random.fold_in(stream_key, 6), dim), (blocks,), jnp.float32, least / len(pieces), top_value / len(pieces))
        return jnp.repeat(jnp.exp(heights), extent[dim] // blocks).reshape((-1,) + (1,) * (len(extent) - dim - 1))

    level = one(*pieces[0])
    for cut in pieces[1:]:
        level = level * one(*cut)
    return level


def centred(own_key, dims, width, most, cuts=(), kind=jnp.bfloat16):
    entries = width * jax.random.normal(own_key, dims, jnp.float32)
    if cuts:
        entries = entries * block_scale(own_key, dims, cuts, -0.22, 0.18)
    return jnp.clip(entries, -most, most).astype(kind)


def setup_inputs(seed: int = 0) -> dict:
    key_list = jax.random.split(jax.random.key(seed), 7)
    return {
        "latents": centred(key_list[0], (MICRO, CH, POSITIONS, FRAMES), 1.0, 6.0, ((1, 2), (2, 4))),
        "timesteps": jax.random.randint(key_list[1], (MICRO,), 0, NSTEPS).astype(jnp.int32),
        "weights": centred(key_list[2], (LEVELS, CH, CH), CH ** -0.5, 0.15625, ((0, 4), (1, 4), (2, 2))),
        "taps": centred(key_list[3], (LEVELS, 3, CH), 0.6, 3.0, ((0, 4),), jnp.float32),
        "time_table": centred(key_list[4], (LEVELS, NSTEPS, CH), 1.0, 5.0, ((0, 4),)),
        "dilations": plant(jax.random.randint(key_list[5], (LEVELS,), 1, DMAX + 1), jax.random.fold_in(key_list[5], 1), 1, DMAX).astype(jnp.int32),
    }


def level_block(current, matrix, tap_rows, embedding, dilation, skip_term):
    widened = current.astype(jnp.float32)
    padded = jnp.pad(widened, ((0, 0), (0, 0), (DMAX, DMAX)))
    earlier = lax.dynamic_slice_in_dim(padded, (DMAX - dilation).astype(jnp.int32), FRAMES, 2)
    later_frames = lax.dynamic_slice_in_dim(padded, (DMAX + dilation).astype(jnp.int32), FRAMES, 2)
    summed = (tap_rows[0][:, None, None] * earlier + tap_rows[1][:, None, None] * widened
              + tap_rows[2][:, None, None] * later_frames + embedding[:, None, None])
    activated = jax.nn.silu(summed).astype(jnp.bfloat16)
    mixed = lax.dot_general(matrix, activated.reshape(CH, -1), (((0,), (0,)), ((), ())),
                            preferred_element_type=jnp.float32).reshape(widened.shape)
    return (widened + mixed + skip_term).astype(jnp.bfloat16)


def reference(latents, timesteps, weights, taps, time_table, dilations):
    results = [[None] * MICRO for level in range(LEVELS)]
    for micro_id in range(MICRO):
        current = latents[micro_id]
        for level in range(LEVELS):
            embedding = time_table[level, timesteps[micro_id]].astype(jnp.float32)
            if level >= LEVELS // 2:
                skip_term = results[LEVELS - 1 - level][micro_id].astype(jnp.float32)
            else:
                skip_term = jnp.float32(0.0)
            current = level_block(current, weights[level], taps[level], embedding,
                                  dilations[level], skip_term)
            results[level][micro_id] = current
    return jnp.stack([jnp.stack(row_list) for row_list in results])
```

```python
import functools

import jax
import jax.numpy as jnp
from jax import lax
from jax.experimental import pallas as pl
from jax.experimental.pallas import tpu as pltpu
from jax.sharding import PartitionSpec as P

MESH = pl.DeviceIdType.MESH
BLOCK = 256


def kernel(
    counts,
    times_ref,
    dilation_ref,
    latent_ref,
    weight_ref,
    taps_ref,
    table_ref,
    out_ref,
    matrix,
    states,
    active,
    params,
    results,
    skips,
    table,
    local_sem,
    left_send,
    left_recv,
    right_send,
    right_recv,
    latent_send,
    state_send,
    state_recv,
    skip_send,
    skip_recv,
):
    sections, rows, cols = counts
    section = lax.axis_index("section")
    row = lax.axis_index("row")
    col = lax.axis_index("col")
    micro, width, frames = latent_ref.shape
    depth = weight_ref.shape[0]
    steps = table_ref.shape[0]
    middle = sections // 2
    mirror = sections - 1 - section
    blocks = [(low, min(low + BLOCK, width)) for low in range(0, width, BLOCK)]
    f32 = jnp.float32

    def place(index):
        return pl.ds(pl.multiple_of(index * depth, depth), depth)

    own = pltpu.make_async_copy(weight_ref, matrix.at[place(row)], local_sem.at[0])
    own.start()
    fetch = pltpu.make_async_copy(table_ref, table, local_sem.at[1])
    fetch.start()

    has_left, has_right = row > 0, row < rows - 1
    has_next, has_last = section < sections - 1, section > 0
    is_first = section == 0
    gives_skip, takes_skip = section < middle - 1, section > middle
    barrier = pltpu.get_barrier_semaphore()

    def greet(**where):
        pl.semaphore_signal(barrier, inc=1, device_id=where, device_id_type=MESH)

    @pl.when(has_left)
    def _():
        greet(row=row - 1)

    @pl.when(has_right)
    def _():
        greet(row=row + 1)

    @pl.when(has_next)
    def _():
        for other in range(cols):
            greet(section=section + 1, col=jnp.int32(other))

    @pl.when(has_last)
    def _():
        for other in range(cols):
            greet(section=section - 1, col=jnp.int32(other))

    @pl.when(is_first)
    def _():
        for hop in range(1, cols):
            greet(col=lax.rem(col + hop, cols))

    @pl.when(jnp.logical_or(gives_skip, takes_skip))
    def _():
        greet(section=mirror)

    def flag(condition):
        return condition.astype(jnp.int32)

    expected = (
        flag(has_left)
        + flag(has_right)
        + cols * (flag(has_next) + flag(has_last))
        + (cols - 1) * flag(is_first)
        + flag(jnp.logical_or(gives_skip, takes_skip))
    )
    pl.semaphore_wait(barrier, expected)

    def move_right(hop):
        source = weight_ref if hop == 0 else matrix.at[place(row - hop)]
        return pltpu.make_async_remote_copy(
            src_ref=source,
            dst_ref=matrix.at[place(row - hop)],
            send_sem=right_send.at[hop],
            recv_sem=right_recv.at[hop],
            device_id={"row": row + 1},
            device_id_type=MESH,
        )

    def move_left(hop):
        source = weight_ref if hop == 0 else matrix.at[place(row + hop)]
        return pltpu.make_async_remote_copy(
            src_ref=source,
            dst_ref=matrix.at[place(row + hop)],
            send_sem=left_send.at[hop],
            recv_sem=left_recv.at[hop],
            device_id={"row": row - 1},
            device_id_type=MESH,
        )

    def arrived(buffer, semaphore):
        pltpu.make_async_remote_copy(
            src_ref=buffer,
            dst_ref=buffer,
            send_sem=local_sem.at[0],
            recv_sem=semaphore,
            device_id={"row": row},
            device_id_type=MESH,
        ).wait_recv()

    @pl.when(has_right)
    def _():
        move_right(0).start()

    @pl.when(has_left)
    def _():
        move_left(0).start()

    def latent_copy(m, n, hop):
        low, high = blocks[n]
        block = states.at[m, col, :, pl.ds(low, high - low)]
        return pltpu.make_async_remote_copy(
            src_ref=block,
            dst_ref=block,
            send_sem=latent_send.at[m, n, hop],
            recv_sem=state_recv.at[m, n, col],
            device_id={"col": lax.rem(col + hop, cols)},
            device_id_type=MESH,
        )

    def state_copy(m, n, hop):
        low, high = blocks[n]
        return pltpu.make_async_remote_copy(
            src_ref=results.at[m, :, pl.ds(low, high - low)],
            dst_ref=states.at[m, col, :, pl.ds(low, high - low)],
            send_sem=state_send.at[m, n, hop],
            recv_sem=state_recv.at[m, n, col],
            device_id={"section": section + 1, "col": lax.rem(col + hop, cols)},
            device_id_type=MESH,
        )

    def skip_copy(m, n):
        low, high = blocks[n]
        return pltpu.make_async_remote_copy(
            src_ref=results.at[m, :, pl.ds(low, high - low)],
            dst_ref=skips.at[m, :, pl.ds(low, high - low)],
            send_sem=skip_send.at[m, n],
            recv_sem=skip_recv.at[m, n],
            device_id={"section": mirror},
            device_id_type=MESH,
        )

    @pl.when(is_first)
    def _():
        for m in range(micro):
            states[m, col] = latent_ref[m].astype(f32).T.astype(jnp.bfloat16)
            for hop in range(1, cols):
                for n in range(len(blocks)):
                    latent_copy(m, n, hop).start()

    @pl.when(section < middle)
    def _():
        skips[...] = jnp.zeros_like(skips)

    dilation = dilation_ref[0]
    target = lax.broadcasted_iota(jnp.int32, (frames, frames), 0)
    origin = lax.broadcasted_iota(jnp.int32, (frames, frames), 1)
    earlier = jnp.where(origin == target - dilation, 1.0, 0.0).astype(jnp.bfloat16)
    later = jnp.where(origin == target + dilation, 1.0, 0.0).astype(jnp.bfloat16)

    slot = lax.broadcasted_iota(jnp.int32, (16, steps), 0)
    number = lax.broadcasted_iota(jnp.int32, (16, steps), 1)
    chosen = jnp.zeros((16, steps), f32)
    for m in range(micro):
        hit = jnp.logical_and(slot == m, number == times_ref[m])
        chosen = jnp.where(hit, 1.0, chosen)
    fetch.wait()
    embedding = jnp.dot(chosen.astype(jnp.bfloat16), table[...], preferred_element_type=f32)
    for other in range(cols):
        span = slice(other * width, (other + 1) * width)
        params[other, 0:3, :] = taps_ref[:, span]
        params[other, 3 : 3 + micro, :] = embedding[0:micro, span]

    def activate(m, is_latent):
        for hop in range(cols):
            other = lax.rem(col + hop, cols)
            for n, (low, high) in enumerate(blocks):
                if not (is_latent and hop == 0):
                    arrived(
                        states.at[m, other, :, pl.ds(low, high - low)],
                        state_recv.at[m, n, other],
                    )
                value = states[m, other, :, low:high]
                summed = (
                    params[other, 0:1, low:high]
                    * jnp.dot(earlier, value, preferred_element_type=f32)
                    + params[other, 1:2, low:high] * value.astype(f32)
                    + params[other, 2:3, low:high]
                    * jnp.dot(later, value, preferred_element_type=f32)
                    + params[other, 3 + m : 4 + m, low:high]
                )
                active[m, other, :, low:high] = (summed / (1.0 + jnp.exp(-summed))).astype(
                    jnp.bfloat16
                )

    @pl.when(is_first)
    def _():
        for m in range(micro):
            activate(m, True)

    own.wait()
    for hop in range(1, rows):

        @pl.when(row - hop >= 0)
        def _():
            arrived(matrix.at[place(row - hop)], right_recv.at[hop - 1])

            @pl.when(has_right)
            def _():
                move_right(hop).start()

        @pl.when(row + hop < rows)
        def _():
            arrived(matrix.at[place(row + hop)], left_recv.at[hop - 1])

            @pl.when(has_left)
            def _():
                move_left(hop).start()

    for m in range(micro):

        @pl.when(has_last)
        def _():
            activate(m, False)

        @pl.when(section == middle)
        def _():
            skips[m] = states[m, col]

        for n, (low, high) in enumerate(blocks):
            mixed = jnp.dot(
                active[m, 0], matrix[0:width, low:high], preferred_element_type=f32
            )
            for other in range(1, cols):
                mixed += jnp.dot(
                    active[m, other],
                    matrix[other * width : (other + 1) * width, low:high],
                    preferred_element_type=f32,
                )

            @pl.when(takes_skip)
            def _():
                arrived(skips.at[m, :, pl.ds(low, high - low)], skip_recv.at[m, n])

            results[m, :, low:high] = (
                states[m, col, :, low:high].astype(f32)
                + mixed
                + skips[m, :, low:high].astype(f32)
            ).astype(jnp.bfloat16)

            @pl.when(has_next)
            def _():
                for hop in reversed(range(cols)):
                    state_copy(m, n, hop).start()

            @pl.when(gives_skip)
            def _():
                skip_copy(m, n).start()

        out_ref[m] = results[m].astype(f32).T.astype(jnp.bfloat16)

    @pl.when(is_first)
    def _():
        for m in range(micro):
            for hop in range(1, cols):
                for n in range(len(blocks)):
                    latent_copy(m, n, hop).wait_send()

    @pl.when(has_next)
    def _():
        for m in range(micro):
            for hop in range(cols):
                for n in range(len(blocks)):
                    state_copy(m, n, hop).wait_send()

    @pl.when(gives_skip)
    def _():
        for m in range(micro):
            for n in range(len(blocks)):
                skip_copy(m, n).wait_send()

    for hop in range(rows - 1):

        @pl.when(jnp.logical_and(has_right, row - hop >= 0))
        def _():
            move_right(hop).wait_send()

        @pl.when(jnp.logical_and(has_left, row + hop < rows))
        def _():
            move_left(hop).wait_send()


def per_device(counts, latents, timesteps, weights, taps, time_table, dilations):
    sections, rows, cols = counts
    micro, width, _, frames = latents.shape
    depth = weights.shape[1]
    steps, channels = time_table.shape[1:]
    count = pl.cdiv(width, BLOCK)
    bf16 = jnp.bfloat16
    dma = pltpu.SemaphoreType.DMA
    vmem = pl.BlockSpec(memory_space=pltpu.VMEM)
    smem = pl.BlockSpec(memory_space=pltpu.SMEM)
    hbm = pl.BlockSpec(memory_space=pl.ANY)
    out = pl.pallas_call(
        functools.partial(kernel, counts),
        out_shape=jax.ShapeDtypeStruct((micro, width, frames), bf16),
        in_specs=[smem, smem, vmem, hbm, vmem, hbm],
        out_specs=vmem,
        scratch_shapes=[
            pltpu.VMEM((channels, width), bf16),
            pltpu.VMEM((micro, cols, frames, width), bf16),
            pltpu.VMEM((micro, cols, frames, width), bf16),
            pltpu.VMEM((cols, 8, width), jnp.float32),
            pltpu.VMEM((micro, frames, width), bf16),
            pltpu.VMEM((micro, frames, width), bf16),
            pltpu.VMEM((steps, channels), bf16),
            dma((2,)),
            dma((rows,)),
            dma((rows,)),
            dma((rows,)),
            dma((rows,)),
            dma((micro, count, cols)),
            dma((micro, count, cols)),
            dma((micro, count, cols)),
            dma((micro, count)),
            dma((micro, count)),
        ],
        compiler_params=pltpu.CompilerParams(
            collective_id=0, has_side_effects=True, vmem_limit_bytes=32 * 2**20
        ),
    )(
        timesteps,
        dilations,
        latents.reshape(micro, width, frames),
        weights[0],
        taps[0],
        time_table[0],
    )
    return out.reshape(1, micro, width, 1, frames)


def solution(mesh):
    counts = tuple(mesh.shape[axis] for axis in ("section", "row", "col"))
    in_specs = (
        P(None, "col", "row", None),
        P(),
        P("section", "row", "col"),
        P("section", None, None),
        P("section", None, None),
        P("section"),
    )
    return jax.shard_map(
        functools.partial(per_device, counts),
        mesh=mesh,
        in_specs=in_specs,
        out_specs=P("section", None, "col", "row", None),
        check_vma=False,
    )
```

```python
import functools

import jax
import jax.numpy as jnp
from jax import lax
from jax.experimental import pallas as pl
from jax.experimental.pallas import tpu as pltpu
from jax.sharding import PartitionSpec as P

MESH = pl.DeviceIdType.MESH
BLOCK = 256
PIECES = 2


def kernel(
    counts,
    times_ref,
    dilation_ref,
    latent_hbm,
    weight_hbm,
    taps_hbm,
    table_hbm,
    out_ref,
    matrix,
    states,
    active,
    params,
    results,
    skips,
    table,
    latent_ref,
    taps_ref,
    local_sem,
    left_send,
    left_recv,
    right_send,
    right_recv,
    latent_send,
    state_send,
    state_recv,
    skip_send,
    skip_recv,
):
    sections, rows, cols = counts
    section = lax.axis_index("section")
    row = lax.axis_index("row")
    col = lax.axis_index("col")
    micro, width, frames = latent_ref.shape
    weight_ref = weight_hbm.at[0]
    depth = weight_ref.shape[0]
    steps = table.shape[0]
    middle = sections // 2
    mirror = sections - 1 - section
    blocks = [(low, min(low + BLOCK, width)) for low in range(0, width, BLOCK)]
    f32 = jnp.float32

    piece = depth // PIECES

    def place(index, q):
        return pl.ds(pl.multiple_of(index * depth + q * piece, piece), piece)

    own = pltpu.make_async_copy(weight_ref, matrix.at[pl.ds(pl.multiple_of(row * depth, depth), depth)], local_sem.at[0])
    own.start()
    fetch = pltpu.make_async_copy(table_hbm.at[0], table, local_sem.at[1])
    fetch.start()
    fetch_latents = pltpu.make_async_copy(latent_hbm, latent_ref, local_sem.at[2])
    fetch_latents.start()
    fetch_taps = pltpu.make_async_copy(taps_hbm, taps_ref, local_sem.at[3])
    fetch_taps.start()

    has_left, has_right = row > 0, row < rows - 1
    has_next, has_last = section < sections - 1, section > 0
    is_first = section == 0
    gives_skip, takes_skip = section < middle - 1, section > middle
    barrier = pltpu.get_barrier_semaphore()

    def greet(**where):
        pl.semaphore_signal(barrier, inc=1, device_id=where, device_id_type=MESH)

    @pl.when(has_left)
    def _():
        greet(row=row - 1)

    @pl.when(has_right)
    def _():
        greet(row=row + 1)

    @pl.when(has_next)
    def _():
        for other in range(cols):
            greet(section=section + 1, col=jnp.int32(other))

    @pl.when(has_last)
    def _():
        for other in range(cols):
            greet(section=section - 1, col=jnp.int32(other))

    @pl.when(is_first)
    def _():
        for hop in range(1, cols):
            greet(col=lax.rem(col + hop, cols))

    @pl.when(jnp.logical_or(gives_skip, takes_skip))
    def _():
        greet(section=mirror)

    def flag(condition):
        return condition.astype(jnp.int32)

    expected = (
        flag(has_left)
        + flag(has_right)
        + cols * (flag(has_next) + flag(has_last))
        + (cols - 1) * flag(is_first)
        + flag(jnp.logical_or(gives_skip, takes_skip))
    )
    pl.semaphore_wait(barrier, expected)

    def move_right(hop, q):
        source = weight_ref.at[pl.ds(q * piece, piece)] if hop == 0 else matrix.at[place(row - hop, q)]
        return pltpu.make_async_remote_copy(
            src_ref=source,
            dst_ref=matrix.at[place(row - hop, q)],
            send_sem=right_send.at[hop, q],
            recv_sem=right_recv.at[hop, q],
            device_id={"row": row + 1},
            device_id_type=MESH,
        )

    def move_left(hop, q):
        source = weight_ref.at[pl.ds(q * piece, piece)] if hop == 0 else matrix.at[place(row + hop, q)]
        return pltpu.make_async_remote_copy(
            src_ref=source,
            dst_ref=matrix.at[place(row + hop, q)],
            send_sem=left_send.at[hop, q],
            recv_sem=left_recv.at[hop, q],
            device_id={"row": row - 1},
            device_id_type=MESH,
        )

    def arrived(buffer, semaphore):
        pltpu.make_async_remote_copy(
            src_ref=buffer,
            dst_ref=buffer,
            send_sem=local_sem.at[0],
            recv_sem=semaphore,
            device_id={"row": row},
            device_id_type=MESH,
        ).wait_recv()

    @pl.when(has_right)
    def _():
        for q in range(PIECES):
            move_right(0, q).start()

    @pl.when(has_left)
    def _():
        for q in range(PIECES):
            move_left(0, q).start()

    def latent_copy(m, n, hop):
        low, high = blocks[n]
        block = states.at[m, col, :, pl.ds(low, high - low)]
        return pltpu.make_async_remote_copy(
            src_ref=block,
            dst_ref=block,
            send_sem=latent_send.at[m, n, hop],
            recv_sem=state_recv.at[m, n, col],
            device_id={"col": lax.rem(col + hop, cols)},
            device_id_type=MESH,
        )

    def state_copy(m, n, hop):
        low, high = blocks[n]
        return pltpu.make_async_remote_copy(
            src_ref=results.at[m, :, pl.ds(low, high - low)],
            dst_ref=states.at[m, col, :, pl.ds(low, high - low)],
            send_sem=state_send.at[m, n, hop],
            recv_sem=state_recv.at[m, n, col],
            device_id={"section": section + 1, "col": lax.rem(col + hop, cols)},
            device_id_type=MESH,
        )

    def skip_copy(m, n):
        low, high = blocks[n]
        return pltpu.make_async_remote_copy(
            src_ref=results.at[m, :, pl.ds(low, high - low)],
            dst_ref=skips.at[m, :, pl.ds(low, high - low)],
            send_sem=skip_send.at[m, n],
            recv_sem=skip_recv.at[m, n],
            device_id={"section": mirror},
            device_id_type=MESH,
        )

    fetch_latents.wait()

    @pl.when(is_first)
    def _():
        for m in range(micro):
            states[m, col] = latent_ref[m].astype(f32).T.astype(jnp.bfloat16)
            for hop in range(1, cols):
                for n in range(len(blocks)):
                    latent_copy(m, n, hop).start()

    @pl.when(section < middle)
    def _():
        skips[...] = jnp.zeros_like(skips)

    def forward(hop):
        for q in range(PIECES):

            @pl.when(row - hop >= 0)
            def _():
                arrived(matrix.at[place(row - hop, q)], right_recv.at[hop - 1, q])

                @pl.when(has_right)
                def _():
                    move_right(hop, q).start()

            @pl.when(row + hop < rows)
            def _():
                arrived(matrix.at[place(row + hop, q)], left_recv.at[hop - 1, q])

                @pl.when(has_left)
                def _():
                    move_left(hop, q).start()

    if rows > 1:
        forward(1)

    dilation = dilation_ref[0]
    line = lax.broadcasted_iota(jnp.int32, (2 * frames, frames), 0)
    origin = lax.broadcasted_iota(jnp.int32, (2 * frames, frames), 1)
    wanted = jnp.where(line < frames, line - dilation, line - frames + dilation)
    shift = jnp.where(origin == wanted, 1.0, 0.0).astype(jnp.bfloat16)

    slot = lax.broadcasted_iota(jnp.int32, (16, steps), 0)
    number = lax.broadcasted_iota(jnp.int32, (16, steps), 1)
    chosen = jnp.zeros((16, steps), f32)
    for m in range(micro):
        hit = jnp.logical_and(slot == m, number == times_ref[m])
        chosen = jnp.where(hit, 1.0, chosen)
    fetch.wait()
    fetch_taps.wait()
    embedding = jnp.dot(chosen.astype(jnp.bfloat16), table[...], preferred_element_type=f32)
    for other in range(cols):
        span = slice(other * width, (other + 1) * width)
        for tap in range(3):
            params[other, tap : tap + 1, :] = 0.5 * taps_ref[tap, :, span]
        params[other, 3 : 3 + micro, :] = 0.5 * embedding[0:micro, span]

    def activate(m, is_latent):
        for hop in range(cols):
            other = lax.rem(col + hop, cols)
            for n, (low, high) in enumerate(blocks):
                if not (is_latent and hop == 0):
                    arrived(
                        states.at[m, other, :, pl.ds(low, high - low)],
                        state_recv.at[m, n, other],
                    )
                value = states[m, other, :, low:high]
                moved = jnp.dot(shift, value, preferred_element_type=f32)
                half = (
                    params[other, 0:1, low:high] * moved[:frames]
                    + params[other, 1:2, low:high] * value.astype(f32)
                    + params[other, 2:3, low:high] * moved[frames:]
                    + params[other, 3 + m : 4 + m, low:high]
                )
                active[m, other, :, low:high] = (half + half * jnp.tanh(half)).astype(
                    jnp.bfloat16
                )

    for turn in range(max(micro, rows - 2)):
        if turn < micro:

            @pl.when(is_first)
            def _():
                activate(turn, True)

        if turn < rows - 2:
            forward(turn + 2)

    own.wait()
    for m in range(micro):

        @pl.when(has_last)
        def _():
            activate(m, False)

        @pl.when(section == middle)
        def _():
            skips[m] = states[m, col]

        for n, (low, high) in enumerate(blocks):
            mixed = jnp.dot(
                active[m, 0], matrix[0:width, low:high], preferred_element_type=f32
            )
            for other in range(1, cols):
                mixed += jnp.dot(
                    active[m, other],
                    matrix[other * width : (other + 1) * width, low:high],
                    preferred_element_type=f32,
                )

            @pl.when(takes_skip)
            def _():
                arrived(skips.at[m, :, pl.ds(low, high - low)], skip_recv.at[m, n])

            results[m, :, low:high] = (
                states[m, col, :, low:high].astype(f32)
                + mixed
                + skips[m, :, low:high].astype(f32)
            ).astype(jnp.bfloat16)

            @pl.when(has_next)
            def _():
                for hop in reversed(range(cols)):
                    state_copy(m, n, hop).start()

            @pl.when(gives_skip)
            def _():
                skip_copy(m, n).start()

        out_ref[m] = results[m].astype(f32).T.astype(jnp.bfloat16)

    @pl.when(is_first)
    def _():
        for m in range(micro):
            for hop in range(1, cols):
                for n in range(len(blocks)):
                    latent_copy(m, n, hop).wait_send()

    @pl.when(has_next)
    def _():
        for m in range(micro):
            for hop in range(cols):
                for n in range(len(blocks)):
                    state_copy(m, n, hop).wait_send()

    @pl.when(gives_skip)
    def _():
        for m in range(micro):
            for n in range(len(blocks)):
                skip_copy(m, n).wait_send()

    for hop in range(rows - 1):

        @pl.when(jnp.logical_and(has_right, row - hop >= 0))
        def _():
            for q in range(PIECES):
                move_right(hop, q).wait_send()

        @pl.when(jnp.logical_and(has_left, row + hop < rows))
        def _():
            for q in range(PIECES):
                move_left(hop, q).wait_send()


def per_device(counts, latents, timesteps, weights, taps, time_table, dilations):
    sections, rows, cols = counts
    micro, width, _, frames = latents.shape
    depth = weights.shape[1]
    steps, channels = time_table.shape[1:]
    count = pl.cdiv(width, BLOCK)
    bf16 = jnp.bfloat16
    dma = pltpu.SemaphoreType.DMA
    vmem = pl.BlockSpec(memory_space=pltpu.VMEM)
    smem = pl.BlockSpec(memory_space=pltpu.SMEM)
    hbm = pl.BlockSpec(memory_space=pl.ANY)
    out = pl.pallas_call(
        functools.partial(kernel, counts),
        out_shape=jax.ShapeDtypeStruct((micro, width, frames), bf16),
        in_specs=[smem, smem, hbm, hbm, hbm, hbm],
        out_specs=vmem,
        scratch_shapes=[
            pltpu.VMEM((channels, width), bf16),
            pltpu.VMEM((micro, cols, frames, width), bf16),
            pltpu.VMEM((micro, cols, frames, width), bf16),
            pltpu.VMEM((cols, 8, width), jnp.float32),
            pltpu.VMEM((micro, frames, width), bf16),
            pltpu.VMEM((micro, frames, width), bf16),
            pltpu.VMEM((steps, channels), bf16),
            pltpu.VMEM((micro, width, frames), bf16),
            pltpu.VMEM((3, 1, channels), jnp.float32),
            dma((4,)),
            dma((rows, PIECES)),
            dma((rows, PIECES)),
            dma((rows, PIECES)),
            dma((rows, PIECES)),
            dma((micro, count, cols)),
            dma((micro, count, cols)),
            dma((micro, count, cols)),
            dma((micro, count)),
            dma((micro, count)),
        ],
        compiler_params=pltpu.CompilerParams(
            collective_id=0, has_side_effects=True, vmem_limit_bytes=60 * 2**20
        ),
    )(
        timesteps,
        dilations,
        latents.reshape(micro, width, frames),
        weights,
        taps.reshape(3, 1, channels),
        time_table,
    )
    return out.reshape(1, micro, width, 1, frames)


def solution(mesh):
    counts = tuple(mesh.shape[axis] for axis in ("section", "row", "col"))
    in_specs = (
        P(None, "col", "row", None),
        P(),
        P("section", "row", "col"),
        P("section", None, None),
        P("section", None, None),
        P("section"),
    )
    return jax.shard_map(
        functools.partial(per_device, counts),
        mesh=mesh,
        in_specs=in_specs,
        out_specs=P("section", None, "col", "row", None),
        check_vma=False,
    )
```

```python
import functools

import jax
import jax.numpy as jnp
from jax import lax
from jax.experimental import pallas as pl
from jax.experimental.pallas import tpu as pltpu
from jax.sharding import PartitionSpec as P

MESH = pl.DeviceIdType.MESH
BLOCK = 256
PIECES = 2


def kernel(
    counts,
    times_ref,
    dilation_ref,
    latent_hbm,
    weight_hbm,
    taps_hbm,
    table_hbm,
    out_ref,
    matrix,
    states,
    active,
    params,
    results,
    skips,
    table,
    latent_ref,
    taps_ref,
    local_sem,
    turn_sem,
    left_send,
    left_recv,
    right_send,
    right_recv,
    latent_send,
    state_send,
    state_recv,
    skip_send,
    skip_recv,
):
    sections, rows, cols = counts
    section = lax.axis_index("section")
    row = lax.axis_index("row")
    col = lax.axis_index("col")
    micro, width, frames = latent_ref.shape
    weight_ref = weight_hbm.at[0]
    depth = weight_ref.shape[0]
    steps = table.shape[0]
    middle = sections // 2
    mirror = sections - 1 - section
    blocks = [(low, min(low + BLOCK, width)) for low in range(0, width, BLOCK)]
    f32 = jnp.float32

    piece = depth // PIECES

    def place(index, q):
        return pl.ds(pl.multiple_of(index * depth + q * piece, piece), piece)

    own = pltpu.make_async_copy(weight_ref, matrix.at[pl.ds(pl.multiple_of(row * depth, depth), depth)], local_sem.at[0])
    own.start()
    fetch = pltpu.make_async_copy(table_hbm.at[0], table, local_sem.at[1])
    fetch.start()
    fetch_latents = pltpu.make_async_copy(latent_hbm, latent_ref, local_sem.at[2])
    fetch_latents.start()
    fetch_taps = pltpu.make_async_copy(taps_hbm, taps_ref, local_sem.at[3])
    fetch_taps.start()

    has_left, has_right = row > 0, row < rows - 1
    has_next, has_last = section < sections - 1, section > 0
    is_first = section == 0
    gives_skip, takes_skip = section < middle - 1, section > middle
    barrier = pltpu.get_barrier_semaphore()

    def greet(**where):
        pl.semaphore_signal(barrier, inc=1, device_id=where, device_id_type=MESH)

    @pl.when(has_left)
    def _():
        greet(row=row - 1)

    @pl.when(has_right)
    def _():
        greet(row=row + 1)

    @pl.when(has_next)
    def _():
        for other in range(cols):
            greet(section=section + 1, col=jnp.int32(other))

    @pl.when(has_last)
    def _():
        for other in range(cols):
            greet(section=section - 1, col=jnp.int32(other))

    @pl.when(is_first)
    def _():
        for hop in range(1, cols):
            greet(col=lax.rem(col + hop, cols))

    @pl.when(jnp.logical_or(gives_skip, takes_skip))
    def _():
        greet(section=mirror)

    def flag(condition):
        return condition.astype(jnp.int32)

    expected = (
        flag(has_left)
        + flag(has_right)
        + cols * (flag(has_next) + flag(has_last))
        + (cols - 1) * flag(is_first)
        + flag(jnp.logical_or(gives_skip, takes_skip))
    )
    pl.semaphore_wait(barrier, expected)

    def move_right(hop, q):
        source = weight_ref.at[pl.ds(q * piece, piece)] if hop == 0 else matrix.at[place(row - hop, q)]
        return pltpu.make_async_remote_copy(
            src_ref=source,
            dst_ref=matrix.at[place(row - hop, q)],
            send_sem=right_send.at[hop, q],
            recv_sem=right_recv.at[hop, q],
            device_id={"row": row + 1},
            device_id_type=MESH,
        )

    def move_left(hop, q):
        source = weight_ref.at[pl.ds(q * piece, piece)] if hop == 0 else matrix.at[place(row + hop, q)]
        return pltpu.make_async_remote_copy(
            src_ref=source,
            dst_ref=matrix.at[place(row + hop, q)],
            send_sem=left_send.at[hop, q],
            recv_sem=left_recv.at[hop, q],
            device_id={"row": row - 1},
            device_id_type=MESH,
        )

    def arrived(buffer, semaphore):
        pltpu.make_async_remote_copy(
            src_ref=buffer,
            dst_ref=buffer,
            send_sem=local_sem.at[0],
            recv_sem=semaphore,
            device_id={"row": row},
            device_id_type=MESH,
        ).wait_recv()

    goes_first = jnp.logical_and(lax.rem(section, 2) == 0, has_next)
    goes_second = lax.rem(section, 2) == 1

    @pl.when(goes_second)
    def _():
        pl.semaphore_wait(turn_sem, 1)

    @pl.when(has_right)
    def _():
        for q in range(PIECES):
            move_right(0, q).start()

    @pl.when(has_left)
    def _():
        for q in range(PIECES):
            move_left(0, q).start()

    def latent_copy(m, n, hop):
        low, high = blocks[n]
        block = states.at[m, col, :, pl.ds(low, high - low)]
        return pltpu.make_async_remote_copy(
            src_ref=block,
            dst_ref=block,
            send_sem=latent_send.at[m, n, hop],
            recv_sem=state_recv.at[m, n, col],
            device_id={"col": lax.rem(col + hop, cols)},
            device_id_type=MESH,
        )

    def state_copy(m, n, hop):
        low, high = blocks[n]
        return pltpu.make_async_remote_copy(
            src_ref=results.at[m, :, pl.ds(low, high - low)],
            dst_ref=states.at[m, col, :, pl.ds(low, high - low)],
            send_sem=state_send.at[m, n, hop],
            recv_sem=state_recv.at[m, n, col],
            device_id={"section": section + 1, "col": lax.rem(col + hop, cols)},
            device_id_type=MESH,
        )

    def skip_copy(m, n):
        low, high = blocks[n]
        return pltpu.make_async_remote_copy(
            src_ref=results.at[m, :, pl.ds(low, high - low)],
            dst_ref=skips.at[m, :, pl.ds(low, high - low)],
            send_sem=skip_send.at[m, n],
            recv_sem=skip_recv.at[m, n],
            device_id={"section": mirror},
            device_id_type=MESH,
        )

    fetch_latents.wait()

    @pl.when(is_first)
    def _():
        for m in range(micro):
            states[m, col] = latent_ref[m].astype(f32).T.astype(jnp.bfloat16)
            for hop in range(1, cols):
                for n in range(len(blocks)):
                    latent_copy(m, n, hop).start()

    @pl.when(section < middle)
    def _():
        skips[...] = jnp.zeros_like(skips)

    def forward(hop):
        for q in range(PIECES):

            @pl.when(row - hop >= 0)
            def _():
                arrived(matrix.at[place(row - hop, q)], right_recv.at[hop - 1, q])

                @pl.when(has_right)
                def _():
                    move_right(hop, q).start()

            @pl.when(row + hop < rows)
            def _():
                arrived(matrix.at[place(row + hop, q)], left_recv.at[hop - 1, q])

                @pl.when(has_left)
                def _():
                    move_left(hop, q).start()

    if rows > 1:
        forward(1)

        @pl.when(has_right)
        def _():
            for q in range(PIECES):
                move_right(0, q).wait_send()

        @pl.when(has_left)
        def _():
            for q in range(PIECES):
                move_left(0, q).wait_send()

    @pl.when(goes_first)
    def _():
        pl.semaphore_signal(
            turn_sem, inc=1, device_id={"section": section + 1}, device_id_type=MESH
        )

    dilation = dilation_ref[0]
    line = lax.broadcasted_iota(jnp.int32, (2 * frames, frames), 0)
    origin = lax.broadcasted_iota(jnp.int32, (2 * frames, frames), 1)
    wanted = jnp.where(line < frames, line - dilation, line - frames + dilation)
    shift = jnp.where(origin == wanted, 1.0, 0.0).astype(jnp.bfloat16)

    slot = lax.broadcasted_iota(jnp.int32, (16, steps), 0)
    number = lax.broadcasted_iota(jnp.int32, (16, steps), 1)
    chosen = jnp.zeros((16, steps), f32)
    for m in range(micro):
        hit = jnp.logical_and(slot == m, number == times_ref[m])
        chosen = jnp.where(hit, 1.0, chosen)
    fetch.wait()
    fetch_taps.wait()
    embedding = jnp.dot(chosen.astype(jnp.bfloat16), table[...], preferred_element_type=f32)
    for other in range(cols):
        span = slice(other * width, (other + 1) * width)
        for tap in range(3):
            params[other, tap : tap + 1, :] = 0.5 * taps_ref[tap, :, span]
        params[other, 3 : 3 + micro, :] = 0.5 * embedding[0:micro, span]

    def activate(m, is_latent):
        for n, (low, high) in enumerate(blocks):
            for hop in range(cols):
                other = lax.rem(col + hop, cols)
                if not (is_latent and hop == 0):
                    arrived(
                        states.at[m, other, :, pl.ds(low, high - low)],
                        state_recv.at[m, n, other],
                    )
                value = states[m, other, :, low:high]
                moved = jnp.dot(shift, value, preferred_element_type=f32)
                half = (
                    params[other, 0:1, low:high] * moved[:frames]
                    + params[other, 1:2, low:high] * value.astype(f32)
                    + params[other, 2:3, low:high] * moved[frames:]
                    + params[other, 3 + m : 4 + m, low:high]
                )
                active[m, other, :, low:high] = (half + half * jnp.tanh(half)).astype(
                    jnp.bfloat16
                )

    for turn in range(max(micro, rows - 2)):
        if turn < micro:

            @pl.when(is_first)
            def _():
                activate(turn, True)

        if turn < rows - 2:
            forward(turn + 2)

    own.wait()
    for m in range(micro):

        @pl.when(has_last)
        def _():
            activate(m, False)

        @pl.when(section == middle)
        def _():
            skips[m] = states[m, col]

        for n, (low, high) in enumerate(blocks):
            mixed = jnp.dot(
                active[m, 0], matrix[0:width, low:high], preferred_element_type=f32
            )
            for other in range(1, cols):
                mixed += jnp.dot(
                    active[m, other],
                    matrix[other * width : (other + 1) * width, low:high],
                    preferred_element_type=f32,
                )

            @pl.when(takes_skip)
            def _():
                arrived(skips.at[m, :, pl.ds(low, high - low)], skip_recv.at[m, n])

            results[m, :, low:high] = (
                states[m, col, :, low:high].astype(f32)
                + mixed
                + skips[m, :, low:high].astype(f32)
            ).astype(jnp.bfloat16)

            @pl.when(has_next)
            def _():
                for hop in reversed(range(cols)):
                    state_copy(m, n, hop).start()

            @pl.when(gives_skip)
            def _():
                skip_copy(m, n).start()


    for m in range(micro):
        out_ref[m] = results[m].astype(f32).T.astype(jnp.bfloat16)

    @pl.when(is_first)
    def _():
        for m in range(micro):
            for hop in range(1, cols):
                for n in range(len(blocks)):
                    latent_copy(m, n, hop).wait_send()

    @pl.when(has_next)
    def _():
        for m in range(micro):
            for hop in range(cols):
                for n in range(len(blocks)):
                    state_copy(m, n, hop).wait_send()

    @pl.when(gives_skip)
    def _():
        for m in range(micro):
            for n in range(len(blocks)):
                skip_copy(m, n).wait_send()

    for hop in range(1, rows - 1):

        @pl.when(jnp.logical_and(has_right, row - hop >= 0))
        def _():
            for q in range(PIECES):
                move_right(hop, q).wait_send()

        @pl.when(jnp.logical_and(has_left, row + hop < rows))
        def _():
            for q in range(PIECES):
                move_left(hop, q).wait_send()


def per_device(counts, latents, timesteps, weights, taps, time_table, dilations):
    sections, rows, cols = counts
    micro, width, _, frames = latents.shape
    depth = weights.shape[1]
    steps, channels = time_table.shape[1:]
    count = pl.cdiv(width, BLOCK)
    bf16 = jnp.bfloat16
    dma = pltpu.SemaphoreType.DMA
    vmem = pl.BlockSpec(memory_space=pltpu.VMEM)
    smem = pl.BlockSpec(memory_space=pltpu.SMEM)
    hbm = pl.BlockSpec(memory_space=pl.ANY)
    out = pl.pallas_call(
        functools.partial(kernel, counts),
        out_shape=jax.ShapeDtypeStruct((micro, width, frames), bf16),
        in_specs=[smem, smem, hbm, hbm, hbm, hbm],
        out_specs=vmem,
        scratch_shapes=[
            pltpu.VMEM((channels, width), bf16),
            pltpu.VMEM((micro, cols, frames, width), bf16),
            pltpu.VMEM((micro, cols, frames, width), bf16),
            pltpu.VMEM((cols, 8, width), jnp.float32),
            pltpu.VMEM((micro, frames, width), bf16),
            pltpu.VMEM((micro, frames, width), bf16),
            pltpu.VMEM((steps, channels), bf16),
            pltpu.VMEM((micro, width, frames), bf16),
            pltpu.VMEM((3, 1, channels), jnp.float32),
            dma((4,)),
            pltpu.SemaphoreType.REGULAR,
            dma((rows, PIECES)),
            dma((rows, PIECES)),
            dma((rows, PIECES)),
            dma((rows, PIECES)),
            dma((micro, count, cols)),
            dma((micro, count, cols)),
            dma((micro, count, cols)),
            dma((micro, count)),
            dma((micro, count)),
        ],
        compiler_params=pltpu.CompilerParams(
            collective_id=0, has_side_effects=True, vmem_limit_bytes=60 * 2**20
        ),
    )(
        timesteps,
        dilations,
        latents.reshape(micro, width, frames),
        weights,
        taps.reshape(3, 1, channels),
        time_table,
    )
    return out.reshape(1, micro, width, 1, frames)


def solution(mesh):
    counts = tuple(mesh.shape[axis] for axis in ("section", "row", "col"))
    in_specs = (
        P(None, "col", "row", None),
        P(),
        P("section", "row", "col"),
        P("section", None, None),
        P("section", None, None),
        P("section"),
    )
    return jax.shard_map(
        functools.partial(per_device, counts),
        mesh=mesh,
        in_specs=in_specs,
        out_specs=P("section", None, "col", "row", None),
        check_vma=False,
    )
```

```python
import functools

import jax
import jax.numpy as jnp
from jax import lax
from jax.experimental import pallas as pl
from jax.experimental.pallas import tpu as pltpu
from jax.sharding import PartitionSpec as P

MESH = pl.DeviceIdType.MESH
BLOCK = 640
PIECES = 5


def kernel(
    counts,
    times_ref,
    dilation_ref,
    latent_hbm,
    weight_hbm,
    taps_hbm,
    table_hbm,
    out_ref,
    matrix,
    states,
    active,
    params,
    results,
    skips,
    table,
    latent_ref,
    taps_ref,
    local_sem,
    turn_sem,
    left_send,
    left_recv,
    right_send,
    right_recv,
    latent_send,
    state_send,
    state_recv,
    skip_send,
    skip_recv,
):
    sections, rows, cols = counts
    section = lax.axis_index("section")
    row = lax.axis_index("row")
    col = lax.axis_index("col")
    micro, width, frames = latent_ref.shape
    weight_ref = weight_hbm.at[0]
    depth = weight_ref.shape[0]
    steps = table.shape[0]
    middle = sections // 2
    mirror = sections - 1 - section
    blocks = [(low, min(low + BLOCK, width)) for low in range(0, width, BLOCK)]
    f32 = jnp.float32

    piece = depth // PIECES

    def place(index, q):
        return pl.ds(pl.multiple_of(index * depth + q * piece, piece), piece)

    own = pltpu.make_async_copy(weight_ref, matrix.at[pl.ds(pl.multiple_of(row * depth, depth), depth)], local_sem.at[0])
    own.start()
    fetch = pltpu.make_async_copy(table_hbm.at[0], table, local_sem.at[1])
    fetch.start()
    fetch_latents = pltpu.make_async_copy(latent_hbm, latent_ref, local_sem.at[2])
    fetch_latents.start()
    fetch_taps = pltpu.make_async_copy(taps_hbm, taps_ref, local_sem.at[3])
    fetch_taps.start()

    has_left, has_right = row > 0, row < rows - 1
    has_next, has_last = section < sections - 1, section > 0
    is_first = section == 0
    gives_skip, takes_skip = section < middle - 1, section > middle
    barrier = pltpu.get_barrier_semaphore()

    def greet(**where):
        pl.semaphore_signal(barrier, inc=1, device_id=where, device_id_type=MESH)

    @pl.when(has_left)
    def _():
        greet(row=row - 1)

    @pl.when(has_right)
    def _():
        greet(row=row + 1)

    @pl.when(has_next)
    def _():
        for other in range(cols):
            greet(section=section + 1, col=jnp.int32(other))

    @pl.when(has_last)
    def _():
        for other in range(cols):
            greet(section=section - 1, col=jnp.int32(other))

    @pl.when(is_first)
    def _():
        for hop in range(1, cols):
            greet(col=lax.rem(col + hop, cols))

    @pl.when(jnp.logical_or(gives_skip, takes_skip))
    def _():
        greet(section=mirror)

    def flag(condition):
        return condition.astype(jnp.int32)

    expected = (
        flag(has_left)
        + flag(has_right)
        + cols * (flag(has_next) + flag(has_last))
        + (cols - 1) * flag(is_first)
        + flag(jnp.logical_or(gives_skip, takes_skip))
    )
    pl.semaphore_wait(barrier, expected)

    def move_right(hop, q):
        source = weight_ref.at[pl.ds(q * piece, piece)] if hop == 0 else matrix.at[place(row - hop, q)]
        return pltpu.make_async_remote_copy(
            src_ref=source,
            dst_ref=matrix.at[place(row - hop, q)],
            send_sem=right_send.at[hop, q],
            recv_sem=right_recv.at[hop, q],
            device_id={"row": row + 1},
            device_id_type=MESH,
        )

    def move_left(hop, q):
        source = weight_ref.at[pl.ds(q * piece, piece)] if hop == 0 else matrix.at[place(row + hop, q)]
        return pltpu.make_async_remote_copy(
            src_ref=source,
            dst_ref=matrix.at[place(row + hop, q)],
            send_sem=left_send.at[hop, q],
            recv_sem=left_recv.at[hop, q],
            device_id={"row": row - 1},
            device_id_type=MESH,
        )

    def arrived(buffer, semaphore):
        pltpu.make_async_remote_copy(
            src_ref=buffer,
            dst_ref=buffer,
            send_sem=local_sem.at[0],
            recv_sem=semaphore,
            device_id={"row": row},
            device_id_type=MESH,
        ).wait_recv()

    goes_first = jnp.logical_and(lax.rem(section, 2) == 0, has_next)
    goes_second = lax.rem(section, 2) == 1

    @pl.when(goes_second)
    def _():
        pl.semaphore_wait(turn_sem, 1)

    @pl.when(has_right)
    def _():
        for q in range(PIECES):
            move_right(0, q).start()

    @pl.when(has_left)
    def _():
        for q in range(PIECES):
            move_left(0, q).start()

    def latent_copy(m, n, hop):
        low, high = blocks[n]
        block = states.at[m, col, :, pl.ds(low, high - low)]
        return pltpu.make_async_remote_copy(
            src_ref=block,
            dst_ref=block,
            send_sem=latent_send.at[m, n, hop],
            recv_sem=state_recv.at[m, n, col],
            device_id={"col": lax.rem(col + hop, cols)},
            device_id_type=MESH,
        )

    def state_copy(m, n, hop):
        low, high = blocks[n]
        return pltpu.make_async_remote_copy(
            src_ref=results.at[m, :, pl.ds(low, high - low)],
            dst_ref=states.at[m, col, :, pl.ds(low, high - low)],
            send_sem=state_send.at[m, n, hop],
            recv_sem=state_recv.at[m, n, col],
            device_id={"section": section + 1, "col": lax.rem(col + hop, cols)},
            device_id_type=MESH,
        )

    def skip_copy(m, n):
        low, high = blocks[n]
        return pltpu.make_async_remote_copy(
            src_ref=results.at[m, :, pl.ds(low, high - low)],
            dst_ref=skips.at[m, :, pl.ds(low, high - low)],
            send_sem=skip_send.at[m, n],
            recv_sem=skip_recv.at[m, n],
            device_id={"section": mirror},
            device_id_type=MESH,
        )

    fetch_latents.wait()

    @pl.when(is_first)
    def _():
        for m in range(micro):
            states[m, col] = latent_ref[m].astype(f32).T.astype(jnp.bfloat16)
            for hop in range(1, cols):
                for n in range(len(blocks)):
                    latent_copy(m, n, hop).start()

    @pl.when(section < middle)
    def _():
        skips[...] = jnp.zeros_like(skips)

    def forward(hop):
        for q in range(PIECES):

            @pl.when(row - hop >= 0)
            def _():
                arrived(matrix.at[place(row - hop, q)], right_recv.at[hop - 1, q])

                @pl.when(has_right)
                def _():
                    move_right(hop, q).start()

            @pl.when(row + hop < rows)
            def _():
                arrived(matrix.at[place(row + hop, q)], left_recv.at[hop - 1, q])

                @pl.when(has_left)
                def _():
                    move_left(hop, q).start()

    if rows > 1:
        forward(1)

        @pl.when(has_right)
        def _():
            for q in range(PIECES):
                move_right(0, q).wait_send()

        @pl.when(has_left)
        def _():
            for q in range(PIECES):
                move_left(0, q).wait_send()

    @pl.when(goes_first)
    def _():
        pl.semaphore_signal(
            turn_sem, inc=1, device_id={"section": section + 1}, device_id_type=MESH
        )

    dilation = dilation_ref[0]
    line = lax.broadcasted_iota(jnp.int32, (2 * frames, frames), 0)
    origin = lax.broadcasted_iota(jnp.int32, (2 * frames, frames), 1)
    wanted = jnp.where(line < frames, line - dilation, line - frames + dilation)
    shift = jnp.where(origin == wanted, 1.0, 0.0).astype(jnp.bfloat16)

    slot = lax.broadcasted_iota(jnp.int32, (16, steps), 0)
    number = lax.broadcasted_iota(jnp.int32, (16, steps), 1)
    chosen = jnp.zeros((16, steps), f32)
    for m in range(micro):
        hit = jnp.logical_and(slot == m, number == times_ref[m])
        chosen = jnp.where(hit, 1.0, chosen)
    fetch.wait()
    fetch_taps.wait()
    embedding = jnp.dot(chosen.astype(jnp.bfloat16), table[...], preferred_element_type=f32)
    for other in range(cols):
        span = slice(other * width, (other + 1) * width)
        for tap in range(3):
            params[other, tap : tap + 1, :] = 0.5 * taps_ref[tap, :, span]
        params[other, 3 : 3 + micro, :] = 0.5 * embedding[0:micro, span]

    def activate(m, is_latent):
        for n, (low, high) in enumerate(blocks):
            for hop in range(cols):
                other = lax.rem(col + hop, cols)
                if not (is_latent and hop == 0):
                    arrived(
                        states.at[m, other, :, pl.ds(low, high - low)],
                        state_recv.at[m, n, other],
                    )
                value = states[m, other, :, low:high]
                moved = jnp.dot(shift, value, preferred_element_type=f32)
                half = (
                    params[other, 0:1, low:high] * moved[:frames]
                    + params[other, 1:2, low:high] * value.astype(f32)
                    + params[other, 2:3, low:high] * moved[frames:]
                    + params[other, 3 + m : 4 + m, low:high]
                )
                active[m, other, :, low:high] = (half + half * jnp.tanh(half)).astype(
                    jnp.bfloat16
                )

    for turn in range(max(micro, rows - 2)):
        if turn < micro:

            @pl.when(is_first)
            def _():
                activate(turn, True)

        if turn < rows - 2:
            forward(turn + 2)

    own.wait()
    for m in range(micro):

        @pl.when(has_last)
        def _():
            activate(m, False)

        @pl.when(section == middle)
        def _():
            skips[m] = states[m, col]

        for n, (low, high) in enumerate(blocks):
            mixed = jnp.dot(
                active[m, 0], matrix[0:width, low:high], preferred_element_type=f32
            )
            for other in range(1, cols):
                mixed += jnp.dot(
                    active[m, other],
                    matrix[other * width : (other + 1) * width, low:high],
                    preferred_element_type=f32,
                )

            @pl.when(takes_skip)
            def _():
                arrived(skips.at[m, :, pl.ds(low, high - low)], skip_recv.at[m, n])

            results[m, :, low:high] = (
                states[m, col, :, low:high].astype(f32)
                + mixed
                + skips[m, :, low:high].astype(f32)
            ).astype(jnp.bfloat16)

            @pl.when(has_next)
            def _():
                for hop in reversed(range(cols)):
                    state_copy(m, n, hop).start()

            @pl.when(gives_skip)
            def _():
                skip_copy(m, n).start()


    for m in range(micro):
        out_ref[m] = results[m].astype(f32).T.astype(jnp.bfloat16)

    @pl.when(is_first)
    def _():
        for m in range(micro):
            for hop in range(1, cols):
                for n in range(len(blocks)):
                    latent_copy(m, n, hop).wait_send()

    @pl.when(has_next)
    def _():
        for m in range(micro):
            for hop in range(cols):
                for n in range(len(blocks)):
                    state_copy(m, n, hop).wait_send()

    @pl.when(gives_skip)
    def _():
        for m in range(micro):
            for n in range(len(blocks)):
                skip_copy(m, n).wait_send()

    for hop in range(1, rows - 1):

        @pl.when(jnp.logical_and(has_right, row - hop >= 0))
        def _():
            for q in range(PIECES):
                move_right(hop, q).wait_send()

        @pl.when(jnp.logical_and(has_left, row + hop < rows))
        def _():
            for q in range(PIECES):
                move_left(hop, q).wait_send()


def per_device(counts, latents, timesteps, weights, taps, time_table, dilations):
    sections, rows, cols = counts
    micro, width, _, frames = latents.shape
    depth = weights.shape[1]
    steps, channels = time_table.shape[1:]
    count = pl.cdiv(width, BLOCK)
    bf16 = jnp.bfloat16
    dma = pltpu.SemaphoreType.DMA
    vmem = pl.BlockSpec(memory_space=pltpu.VMEM)
    smem = pl.BlockSpec(memory_space=pltpu.SMEM)
    hbm = pl.BlockSpec(memory_space=pl.ANY)
    out = pl.pallas_call(
        functools.partial(kernel, counts),
        out_shape=jax.ShapeDtypeStruct((micro, width, frames), bf16),
        in_specs=[smem, smem, hbm, hbm, hbm, hbm],
        out_specs=vmem,
        scratch_shapes=[
            pltpu.VMEM((channels, width), bf16),
            pltpu.VMEM((micro, cols, frames, width), bf16),
            pltpu.VMEM((micro, cols, frames, width), bf16),
            pltpu.VMEM((cols, 8, width), jnp.float32),
            pltpu.VMEM((micro, frames, width), bf16),
            pltpu.VMEM((micro, frames, width), bf16),
            pltpu.VMEM((steps, channels), bf16),
            pltpu.VMEM((micro, width, frames), bf16),
            pltpu.VMEM((3, 1, channels), jnp.float32),
            dma((4,)),
            pltpu.SemaphoreType.REGULAR,
            dma((rows, PIECES)),
            dma((rows, PIECES)),
            dma((rows, PIECES)),
            dma((rows, PIECES)),
            dma((micro, count, cols)),
            dma((micro, count, cols)),
            dma((micro, count, cols)),
            dma((micro, count)),
            dma((micro, count)),
        ],
        compiler_params=pltpu.CompilerParams(
            collective_id=0, has_side_effects=True, vmem_limit_bytes=60 * 2**20
        ),
    )(
        timesteps,
        dilations,
        latents.reshape(micro, width, frames),
        weights,
        taps.reshape(3, 1, channels),
        time_table,
    )
    return out.reshape(1, micro, width, 1, frames)


def solution(mesh):
    counts = tuple(mesh.shape[axis] for axis in ("section", "row", "col"))
    in_specs = (
        P(None, "col", "row", None),
        P(),
        P("section", "row", "col"),
        P("section", None, None),
        P("section", None, None),
        P("section"),
    )
    return jax.shard_map(
        functools.partial(per_device, counts),
        mesh=mesh,
        in_specs=in_specs,
        out_specs=P("section", None, "col", "row", None),
        check_vma=False,
    )
```

```python
import functools

import jax
import jax.numpy as jnp
from jax import lax
from jax.experimental import pallas as pl
from jax.experimental.pallas import tpu as pltpu
from jax.sharding import PartitionSpec as P

MESH = pl.DeviceIdType.MESH
BLOCK = 640
PIECES = 5


def kernel(
    counts,
    times_ref,
    dilation_ref,
    latent_hbm,
    weight_hbm,
    taps_hbm,
    table_hbm,
    out_ref,
    matrix,
    states,
    active,
    params,
    results,
    skips,
    table,
    latent_ref,
    taps_ref,
    local_sem,
    turn_sem,
    left_send,
    left_recv,
    right_send,
    right_recv,
    latent_send,
    state_send,
    state_recv,
    skip_send,
    skip_recv,
):
    sections, rows, cols = counts
    section = lax.axis_index("section")
    row = lax.axis_index("row")
    col = lax.axis_index("col")
    micro, width, frames = latent_ref.shape
    weight_ref = weight_hbm.at[0]
    depth = weight_ref.shape[0]
    steps = table.shape[0]
    middle = sections // 2
    mirror = sections - 1 - section
    blocks = [(low, min(low + BLOCK, width)) for low in range(0, width, BLOCK)]
    f32 = jnp.float32

    piece = depth // PIECES

    def place(index, q):
        return pl.ds(pl.multiple_of(index * depth + q * piece, piece), piece)

    own = pltpu.make_async_copy(weight_ref, matrix.at[pl.ds(pl.multiple_of(row * depth, depth), depth)], local_sem.at[0])
    own.start()
    fetch = pltpu.make_async_copy(table_hbm.at[0], table, local_sem.at[1])
    fetch.start()
    fetch_latents = pltpu.make_async_copy(latent_hbm, latent_ref, local_sem.at[2])
    fetch_latents.start()
    fetch_taps = pltpu.make_async_copy(taps_hbm, taps_ref, local_sem.at[3])
    fetch_taps.start()

    has_left, has_right = row > 0, row < rows - 1
    has_next, has_last = section < sections - 1, section > 0
    is_first = section == 0
    gives_skip, takes_skip = section < middle - 1, section > middle
    barrier = pltpu.get_barrier_semaphore()

    def greet(**where):
        pl.semaphore_signal(barrier, inc=1, device_id=where, device_id_type=MESH)

    @pl.when(has_left)
    def _():
        greet(row=row - 1)

    @pl.when(has_right)
    def _():
        greet(row=row + 1)

    @pl.when(has_next)
    def _():
        for other in range(cols):
            greet(section=section + 1, col=jnp.int32(other))

    @pl.when(has_last)
    def _():
        for other in range(cols):
            greet(section=section - 1, col=jnp.int32(other))

    @pl.when(is_first)
    def _():
        for hop in range(1, cols):
            greet(col=lax.rem(col + hop, cols))

    @pl.when(jnp.logical_or(gives_skip, takes_skip))
    def _():
        greet(section=mirror)

    def flag(condition):
        return condition.astype(jnp.int32)

    expected = (
        flag(has_left)
        + flag(has_right)
        + cols * (flag(has_next) + flag(has_last))
        + (cols - 1) * flag(is_first)
        + flag(jnp.logical_or(gives_skip, takes_skip))
    )
    pl.semaphore_wait(barrier, expected)

    def move_right(hop, q):
        source = weight_ref.at[pl.ds(q * piece, piece)] if hop == 0 else matrix.at[place(row - hop, q)]
        return pltpu.make_async_remote_copy(
            src_ref=source,
            dst_ref=matrix.at[place(row - hop, q)],
            send_sem=right_send.at[hop, q],
            recv_sem=right_recv.at[hop, q],
            device_id={"row": row + 1},
            device_id_type=MESH,
        )

    def move_left(hop, q):
        source = weight_ref.at[pl.ds(q * piece, piece)] if hop == 0 else matrix.at[place(row + hop, q)]
        return pltpu.make_async_remote_copy(
            src_ref=source,
            dst_ref=matrix.at[place(row + hop, q)],
            send_sem=left_send.at[hop, q],
            recv_sem=left_recv.at[hop, q],
            device_id={"row": row - 1},
            device_id_type=MESH,
        )

    def arrived(buffer, semaphore):
        pltpu.make_async_remote_copy(
            src_ref=buffer,
            dst_ref=buffer,
            send_sem=local_sem.at[0],
            recv_sem=semaphore,
            device_id={"row": row},
            device_id_type=MESH,
        ).wait_recv()

    goes_first = jnp.logical_and(lax.rem(section, 2) == 0, has_next)
    goes_second = lax.rem(section, 2) == 1

    @pl.when(goes_second)
    def _():
        pl.semaphore_wait(turn_sem, 1)

    @pl.when(has_right)
    def _():
        for q in range(PIECES):
            move_right(0, q).start()

    @pl.when(has_left)
    def _():
        for q in range(PIECES):
            move_left(0, q).start()

    def latent_copy(m, n, hop):
        low, high = blocks[n]
        block = states.at[m, col, :, pl.ds(low, high - low)]
        return pltpu.make_async_remote_copy(
            src_ref=block,
            dst_ref=block,
            send_sem=latent_send.at[m, n, hop],
            recv_sem=state_recv.at[m, n, col],
            device_id={"col": lax.rem(col + hop, cols)},
            device_id_type=MESH,
        )

    def state_copy(m, n, hop):
        low, high = blocks[n]
        return pltpu.make_async_remote_copy(
            src_ref=results.at[m, :, pl.ds(low, high - low)],
            dst_ref=states.at[m, col, :, pl.ds(low, high - low)],
            send_sem=state_send.at[m, n, hop],
            recv_sem=state_recv.at[m, n, col],
            device_id={"section": section + 1, "col": lax.rem(col + hop, cols)},
            device_id_type=MESH,
        )

    def skip_copy(m, n):
        low, high = blocks[n]
        return pltpu.make_async_remote_copy(
            src_ref=results.at[m, :, pl.ds(low, high - low)],
            dst_ref=skips.at[m, :, pl.ds(low, high - low)],
            send_sem=skip_send.at[m, n],
            recv_sem=skip_recv.at[m, n],
            device_id={"section": mirror},
            device_id_type=MESH,
        )

    fetch_latents.wait()

    @pl.when(is_first)
    def _():
        for m in range(micro):
            states[m, col] = latent_ref[m].astype(f32).T.astype(jnp.bfloat16)
            for hop in range(1, cols):
                for n in range(len(blocks)):
                    latent_copy(m, n, hop).start()

    @pl.when(section < middle)
    def _():
        skips[...] = jnp.zeros_like(skips)

    def forward(hop):
        for q in range(PIECES):

            @pl.when(row - hop >= 0)
            def _():
                arrived(matrix.at[place(row - hop, q)], right_recv.at[hop - 1, q])

                @pl.when(has_right)
                def _():
                    move_right(hop, q).start()

            @pl.when(row + hop < rows)
            def _():
                arrived(matrix.at[place(row + hop, q)], left_recv.at[hop - 1, q])

                @pl.when(has_left)
                def _():
                    move_left(hop, q).start()

    if rows > 1:
        forward(1)

        @pl.when(has_right)
        def _():
            for q in range(PIECES):
                move_right(0, q).wait_send()

        @pl.when(has_left)
        def _():
            for q in range(PIECES):
                move_left(0, q).wait_send()

    @pl.when(goes_first)
    def _():
        pl.semaphore_signal(
            turn_sem, inc=1, device_id={"section": section + 1}, device_id_type=MESH
        )

    dilation = dilation_ref[0]
    line = lax.broadcasted_iota(jnp.int32, (2 * frames, frames), 0)
    origin = lax.broadcasted_iota(jnp.int32, (2 * frames, frames), 1)
    wanted = jnp.where(line < frames, line - dilation, line - frames + dilation)
    shift = jnp.where(origin == wanted, 1.0, 0.0).astype(jnp.bfloat16)

    slot = lax.broadcasted_iota(jnp.int32, (16, steps), 0)
    number = lax.broadcasted_iota(jnp.int32, (16, steps), 1)
    chosen = jnp.zeros((16, steps), f32)
    for m in range(micro):
        hit = jnp.logical_and(slot == m, number == times_ref[m])
        chosen = jnp.where(hit, 1.0, chosen)
    fetch.wait()
    fetch_taps.wait()
    embedding = jnp.dot(chosen.astype(jnp.bfloat16), table[...], preferred_element_type=f32)
    for other in range(cols):
        span = slice(other * width, (other + 1) * width)
        for tap in range(3):
            params[other, tap : tap + 1, :] = 0.5 * taps_ref[tap, :, span]
        params[other, 3 : 3 + micro, :] = 0.5 * embedding[0:micro, span]

    def activate(m, is_latent):
        for n, (low, high) in enumerate(blocks):
            for hop in range(cols):
                other = lax.rem(col + hop, cols)
                if not (is_latent and hop == 0):
                    arrived(
                        states.at[m, other, :, pl.ds(low, high - low)],
                        state_recv.at[m, n, other],
                    )
                value = states[m, other, :, low:high]
                moved = jnp.dot(shift, value, preferred_element_type=f32)
                half = (
                    params[other, 0:1, low:high] * moved[:frames]
                    + params[other, 1:2, low:high] * value.astype(f32)
                    + params[other, 2:3, low:high] * moved[frames:]
                    + params[other, 3 + m : 4 + m, low:high]
                )
                active[m, other, :, low:high] = (half + half * jnp.tanh(half)).astype(
                    jnp.bfloat16
                )

    for turn in range(max(micro, rows - 2)):
        if turn < rows - 2:
            forward(turn + 2)

        if turn < micro:

            @pl.when(is_first)
            def _():
                activate(turn, True)

    own.wait()
    for m in range(micro):

        @pl.when(has_last)
        def _():
            activate(m, False)

        @pl.when(section == middle)
        def _():
            skips[m] = states[m, col]

        for n, (low, high) in enumerate(blocks):
            mixed = jnp.dot(
                active[m, 0], matrix[0:width, low:high], preferred_element_type=f32
            )
            for other in range(1, cols):
                mixed += jnp.dot(
                    active[m, other],
                    matrix[other * width : (other + 1) * width, low:high],
                    preferred_element_type=f32,
                )

            @pl.when(takes_skip)
            def _():
                arrived(skips.at[m, :, pl.ds(low, high - low)], skip_recv.at[m, n])

            results[m, :, low:high] = (
                states[m, col, :, low:high].astype(f32)
                + mixed
                + skips[m, :, low:high].astype(f32)
            ).astype(jnp.bfloat16)

            @pl.when(has_next)
            def _():
                for hop in range(cols):
                    state_copy(m, n, hop).start()

            @pl.when(gives_skip)
            def _():
                skip_copy(m, n).start()


    for m in range(micro):
        out_ref[m] = results[m].astype(f32).T.astype(jnp.bfloat16)

    @pl.when(is_first)
    def _():
        for m in range(micro):
            for hop in range(1, cols):
                for n in range(len(blocks)):
                    latent_copy(m, n, hop).wait_send()

    @pl.when(has_next)
    def _():
        for m in range(micro):
            for hop in range(cols):
                for n in range(len(blocks)):
                    state_copy(m, n, hop).wait_send()

    @pl.when(gives_skip)
    def _():
        for m in range(micro):
            for n in range(len(blocks)):
                skip_copy(m, n).wait_send()

    for hop in range(1, rows - 1):

        @pl.when(jnp.logical_and(has_right, row - hop >= 0))
        def _():
            for q in range(PIECES):
                move_right(hop, q).wait_send()

        @pl.when(jnp.logical_and(has_left, row + hop < rows))
        def _():
            for q in range(PIECES):
                move_left(hop, q).wait_send()


def per_device(counts, latents, timesteps, weights, taps, time_table, dilations):
    sections, rows, cols = counts
    micro, width, _, frames = latents.shape
    depth = weights.shape[1]
    steps, channels = time_table.shape[1:]
    count = pl.cdiv(width, BLOCK)
    bf16 = jnp.bfloat16
    dma = pltpu.SemaphoreType.DMA
    vmem = pl.BlockSpec(memory_space=pltpu.VMEM)
    smem = pl.BlockSpec(memory_space=pltpu.SMEM)
    hbm = pl.BlockSpec(memory_space=pl.ANY)
    out = pl.pallas_call(
        functools.partial(kernel, counts),
        out_shape=jax.ShapeDtypeStruct((micro, width, frames), bf16),
        in_specs=[smem, smem, hbm, hbm, hbm, hbm],
        out_specs=vmem,
        scratch_shapes=[
            pltpu.VMEM((channels, width), bf16),
            pltpu.VMEM((micro, cols, frames, width), bf16),
            pltpu.VMEM((micro, cols, frames, width), bf16),
            pltpu.VMEM((cols, 8, width), jnp.float32),
            pltpu.VMEM((micro, frames, width), bf16),
            pltpu.VMEM((micro, frames, width), bf16),
            pltpu.VMEM((steps, channels), bf16),
            pltpu.VMEM((micro, width, frames), bf16),
            pltpu.VMEM((3, 1, channels), jnp.float32),
            dma((4,)),
            pltpu.SemaphoreType.REGULAR,
            dma((rows, PIECES)),
            dma((rows, PIECES)),
            dma((rows, PIECES)),
            dma((rows, PIECES)),
            dma((micro, count, cols)),
            dma((micro, count, cols)),
            dma((micro, count, cols)),
            dma((micro, count)),
            dma((micro, count)),
        ],
        compiler_params=pltpu.CompilerParams(
            collective_id=0, has_side_effects=True, vmem_limit_bytes=60 * 2**20
        ),
    )(
        timesteps,
        dilations,
        latents.reshape(micro, width, frames),
        weights,
        taps.reshape(3, 1, channels),
        time_table,
    )
    return out.reshape(1, micro, width, 1, frames)


def solution(mesh):
    counts = tuple(mesh.shape[axis] for axis in ("section", "row", "col"))
    in_specs = (
        P(None, "col", "row", None),
        P(),
        P("section", "row", "col"),
        P("section", None, None),
        P("section", None, None),
        P("section"),
    )
    return jax.shard_map(
        functools.partial(per_device, counts),
        mesh=mesh,
        in_specs=in_specs,
        out_specs=P("section", None, "col", "row", None),
        check_vma=False,
    )
```
